32 devices in a mesh: gx: 4 (over x, core), gy: 8 (over z, y).
Axes of the slice: x: 2, y: 2, z: 4, core: 2. Of those that a mesh axis runs over, the one named last changes fastest.
Arguments:
- electric: float32 [3, 64, 128, 256], P(None, 'gx', 'gy'), may hold values from -6 to 6
- magnetic: float32 [3, 64, 128, 256], P(None, 'gx', 'gy'), may hold values from -6 to 6
- aux_electric: float32 [6, 64, 128, 256], P(None, 'gx', 'gy'), may hold values from -3 to 3
- aux_magnetic: float32 [6, 64, 128, 256], P(None, 'gx', 'gy'), may hold values from -3 to 3
- grades: int32 [3, 64, 128, 256], P(None, 'gx', 'gy'), may hold values from 0 to 3
- permittivity: float32 [64, 128, 256], P('gx', 'gy'), may hold values from 1 to 8
- dipole_cell: int32 [3, 16384], P(None, ('gx', 'gy')), may hold values from 0 to 255, as said below
- dipole_port: int32 [16384], P(('gx', 'gy')), may hold values from 0 to 511
- live_count: int32 [32], P(('gx', 'gy')), may hold values from 1 to 512, as said below
- injection: bfloat16 [16384, 512], P(('gx', 'gy')), may hold values from -0.25 to 0.25
- waveform: bfloat16 [512, 16], replicated, may hold values from -6 to 6
Outputs:
- electric_out: float32 [3, 64, 128, 256], P(None, 'gx', 'gy')
- magnetic_out: float32 [3, 64, 128, 256], P(None, 'gx', 'gy')
- port_power: float32 [16, 512], replicated
The draws below stay inside these ranges and needn't reach their ends.
Inputs may be any that keep to these rules, and one draw needn't show every extreme that they name: `dipole_cell`: slot s lies in the block of cells held by the device that holds slot s. The live slots of a device are its first live_count ones; some device has all 512 live.
All inputs are finite; a program needn't handle non-finite values.
Results may differ from the reference program's by a relative error of at most 0.0003.
Values sent between devices are 32-bit elements; how exact they have to be, the bound alone decides.
A program may use at most 128 MiB of HBM per device.

```python
import math
import jax
import jax.numpy as jnp
from jax import lax

CX = 16
CY = 16
NZ = 256
DIP_DEV = 512
STEPS = 16
PORTS = 512
NX = 64
NY = 128
DIPOLES = 16384


def draw_dipole_cell(key, part):
    across = NY // CY
    slots = jnp.arange(DIPOLES, dtype=jnp.int32)
    owner = slots // DIP_DEV
    row_block = owner // across
    col_block = owner % across
    key_x, key_y, key_z = jax.random.split(jax.random.fold_in(key, 11), 3)
    coord_x = row_block * CX + jax.random.randint(key_x, (DIPOLES,), 0, CX)
    coord_y = col_block * CY + jax.random.randint(key_y, (DIPOLES,), 0, CY)
    coord_z = jax.random.randint(key_z, (DIPOLES,), 0, NZ)
    return jnp.stack([coord_x, coord_y, coord_z]).astype(jnp.int32)


def draw_dipole_port(key, part):
    devices = DIPOLES // DIP_DEV
    share = PORTS // devices
    slots = jnp.arange(DIPOLES, dtype=jnp.int32)
    owner = slots // DIP_DEV
    key_near, key_far, key_pick = jax.random.split(jax.random.fold_in(key, 23), 3)
    near = owner * share + jax.random.randint(key_near, (DIPOLES,), 0, share)
    far = jax.random.randint(key_far, (DIPOLES,), 0, PORTS)
    pick = jax.random.randint(key_pick, (DIPOLES,), 0, 4)
    return jnp.where(pick == 0, far, near).astype(jnp.int32)


def draw_live_count(key, part):
    devices = DIPOLES // DIP_DEV
    key_one, key_two, key_full = jax.random.split(jax.random.fold_in(key, 37), 3)
    first = jax.random.randint(key_one, (devices,), 1, DIP_DEV + 1)
    second = jax.random.randint(key_two, (devices,), 1, DIP_DEV + 1)
    counts = jnp.minimum(first, second)
    full = jax.random.randint(key_full, (), 0, devices)
    return jnp.where(jnp.arange(devices) == full, DIP_DEV, counts).astype(jnp.int32)


def place_ends(values, own_key, least, top_value):
    spot = [jax.random.randint(jax.random.fold_in(own_key, axis), (), 0, length) for axis, length in enumerate(values.shape)]
    main_axis = values.shape.index(max(values.shape))
    next_to = spot[:main_axis] + [(spot[main_axis] + 1) % values.shape[main_axis]] + spot[main_axis + 1:]
    return values.at[tuple(spot)].set(least).at[tuple(next_to)].set(top_value)


def block_levels(rng, extent, cuts, least, top_value):
    loudness = 1.0
    for dim, blocks in cuts:
        steps = jax.random.uniform(jax.random.fold_in(jax.random.fold_in(rng, 6), dim), (blocks,), jnp.float32, least / len(cuts), top_value / len(cuts))
        loudness = loudness * jnp.repeat(jnp.exp(steps), extent[dim] // blocks).reshape((-1,) + (1,) * (len(extent) - 1 - dim))
    return loudness


def normal_values(rng, shape, width, limit, cuts=(), kind=jnp.bfloat16):
    values = jax.random.normal(rng, shape, jnp.float32) * width
    if len(cuts) > 0:
        values = block_levels(rng, shape, cuts, -0.22, 0.18) * values
    return jnp.clip(values, min=-limit, max=limit).astype(kind)


def setup_inputs(seed: int = 0) -> dict:
    keys = jax.random.split(jax.random.key(seed), 12)
    electric = normal_values(keys[0], (3, NX, NY, NZ), 1.0, 6.0, ((1, 4), (2, 8)), jnp.float32)
    magnetic = normal_values(keys[1], (3, NX, NY, NZ), 1.0, 6.0, ((1, 4), (2, 8)), jnp.float32)
    aux_electric = normal_values(keys[2], (6, NX, NY, NZ), 0.4, 3.0, ((1, 4), (2, 8)), jnp.float32)
    aux_magnetic = normal_values(keys[3], (6, NX, NY, NZ), 0.4, 3.0, ((1, 4), (2, 8)), jnp.float32)
    grades = place_ends(jax.random.randint(keys[4], (3, NX, NY, NZ), 0, 4), jax.random.fold_in(keys[4], 1), 0, 3).astype(jnp.int32)
    permittivity = jnp.clip(jnp.exp(math.log(8.0) - 2.0794415 * jax.random.uniform(keys[5], (NX, NY, NZ), jnp.float32) ** block_levels(keys[5], (NX, NY, NZ), ((0, 4), (1, 8)), -0.2, 0.2)), 1.0, 8.0)
    dipole_cell = draw_dipole_cell(jax.random.fold_in(keys[11], 71), 0)
    dipole_port = draw_dipole_port(jax.random.fold_in(keys[11], 71), 0)
    live_count = draw_live_count(jax.random.fold_in(keys[11], 71), 0)
    injection = normal_values(keys[9], (DIPOLES, PORTS), PORTS ** -0.5, 0.25, ((0, 32),))
    waveform = normal_values(keys[10], (PORTS, STEPS), 1.0, 6.0)
    return dict(electric=electric, magnetic=magnetic, aux_electric=aux_electric, aux_magnetic=aux_magnetic, grades=grades, permittivity=permittivity, dipole_cell=dipole_cell, dipole_port=dipole_port, live_count=live_count, injection=injection, waveform=waveform)


courant = 0.55
absorb_keep = (0.0, 0.92, 0.75, 0.45)
absorb_take = (0.0, -0.06, -0.18, -0.35)
derivative_pairs = ((2, 1), (1, 2), (0, 2), (2, 0), (1, 0), (0, 1))


def difference(values, axis, plane, forward):
    length = values.shape[axis]
    if plane is None:
        shape = list(values.shape)
        shape[axis] = 1
        plane = jnp.zeros(shape, values.dtype)
    if forward:
        after = jnp.concatenate([lax.slice_in_dim(values, 1, length, axis=axis), plane], axis)
        return after - values
    before = jnp.concatenate([plane, lax.slice_in_dim(values, 0, length - 1, axis=axis)], axis)
    return values - before


def grade_table(grades, table):
    result = jnp.zeros(grades.shape, jnp.float32)
    for level in range(1, 4):
        result = result + jnp.where(grades == level, table[level], 0.0)
    return result


def curl(field, auxiliary, keep, take, planes, forward):
    terms = []
    updated = []
    for number, (component, axis) in enumerate(derivative_pairs):
        plane = None
        if planes is not None and axis == 0:
            plane = planes[0][component - 1]
        if planes is not None and axis == 1:
            plane = planes[1][component // 2]
        slope = difference(field[component], axis, plane, forward)
        carried = keep[axis] * auxiliary[number] + take[axis] * slope
        terms.append(slope + carried)
        updated.append(carried)
    rotation = jnp.stack([terms[0] - terms[1], terms[2] - terms[3], terms[4] - terms[5]])
    return rotation, jnp.stack(updated)


def reference(electric, magnetic, aux_electric, aux_magnetic, grades, permittivity, dipole_cell, dipole_port, live_count, injection, waveform):
    keep = grade_table(grades, absorb_keep)
    take = grade_table(grades, absorb_take)
    slots = jnp.arange(DIPOLES, dtype=jnp.int32)
    live = ((slots % DIP_DEV) < live_count[slots // DIP_DEV]).astype(jnp.float32)
    current = jnp.dot(injection, waveform, preferred_element_type=jnp.float32) * live[:, None]
    flat_cell = (dipole_cell[0] * (NY * NZ) + dipole_cell[1] * NZ + dipole_cell[2]).astype(jnp.int32)
    factor = courant / permittivity
    powers = []
    for step in range(STEPS):
        rotation, aux_electric = curl(electric, aux_electric, keep, take, None, True)
        magnetic = magnetic - courant * rotation
        rotation, aux_magnetic = curl(magnetic, aux_magnetic, keep, take, None, False)
        electric = electric + factor * rotation
        current_now = current[:, step]
        flat_z = electric[2].reshape(-1).at[flat_cell].add(-courant * current_now)
        drive = current_now * flat_z[flat_cell]
        electric = jnp.concatenate([electric[0:2], flat_z.reshape(1, NX, NY, NZ)], 0)
        powers.append(jax.ops.segment_sum(drive, dipole_port, PORTS))
    return electric, magnetic, jnp.stack(powers)
```

```python
import functools

import jax
import jax.numpy as jnp
from jax import lax
from jax.experimental import pallas as pl
from jax.experimental.pallas import tpu as pltpu
from jax.sharding import PartitionSpec as P

MESH = pl.DeviceIdType.MESH
courant = 0.55
absorb_keep = (0.0, 0.92, 0.75, 0.45)
absorb_take = (0.0, -0.06, -0.18, -0.35)
derivative_pairs = ((2, 1), (1, 2), (0, 2), (2, 0), (1, 0), (0, 1))
UNROLL = 4


def grade_table(grades, table):
    result = jnp.where(grades == 1, table[1], 0.0)
    result = jnp.where(grades == 2, table[2], result)
    return jnp.where(grades == 3, table[3], result)


def split_two(values):
    high = values.astype(jnp.bfloat16)
    low = (values - high.astype(jnp.float32)).astype(jnp.bfloat16)
    return high, low


def kernel(
    e_in, h_in, me_in, mh_in, grades_ref, eps_ref, cell_ref, port_ref, live_ref, inj_ref, wave_ref,
    e_out, h_out, power_ref,
    ef, hf, me, mh, keep, take, factor, source,
    send_e, recv_e, send_h, recv_h, cell_t, cell_f, depth_t, depth, current, record,
    load_sem, store_sem, send_sem, recv_sem,
):
    depth_x, depth_y, depth_z = eps_ref.shape
    ports, slots = inj_ref.shape[1], inj_ref.shape[0]
    steps = wave_ref.shape[0]
    ix, iy = lax.axis_index("gx"), lax.axis_index("gy")
    count_x, count_y = lax.axis_size("gx"), lax.axis_size("gy")
    has_left, has_right = ix > 0, ix < count_x - 1
    has_down, has_up = iy > 0, iy < count_y - 1

    loads = [
        pltpu.make_async_copy(e_in, ef.at[:, pl.ds(0, depth_x)], load_sem.at[0]),
        pltpu.make_async_copy(h_in, hf.at[:, pl.ds(1, depth_x)], load_sem.at[1]),
        pltpu.make_async_copy(me_in, me, load_sem.at[2]),
        pltpu.make_async_copy(mh_in, mh, load_sem.at[3]),
    ]
    for copy in loads:
        copy.start()

    plane = jnp.zeros((depth_y, depth_z), jnp.float32)
    for component in (1, 2):
        ef[component, depth_x] = plane
        hf[component, 0] = plane
    recv_e[...] = jnp.zeros(recv_e.shape, jnp.float32)
    recv_h[...] = jnp.zeros(recv_h.shape, jnp.float32)

    barrier = pltpu.get_barrier_semaphore()
    for present, dx, dy in (
        (has_left, -1, 0), (has_right, 1, 0), (has_down, 0, -1), (has_up, 0, 1)
    ):
        @pl.when(present)
        def _(dx=dx, dy=dy):
            pl.semaphore_signal(
                barrier, inc=1, device_id=(ix + dx, iy + dy), device_id_type=MESH
            )

    cells = (cell_ref[0:1, :] - ix * depth_x) * depth_y + (cell_ref[1:2, :] - iy * depth_y)
    hit = lax.broadcasted_iota(jnp.int32, cell_f.shape, 0) == cells
    cell_f[...] = jnp.where(hit, 1.0, 0.0)
    cell_t[...] = jnp.where(hit, 1.0, 0.0).astype(jnp.bfloat16)
    hit = lax.broadcasted_iota(jnp.int32, depth_t.shape, 0) == cell_ref[2:3, :]
    table = jnp.where(hit, 1.0, 0.0)
    depth_t[...] = table.astype(jnp.bfloat16)
    depth[...] = table.T.astype(jnp.bfloat16)
    live = lax.broadcasted_iota(jnp.int32, (1, slots), 1) < live_ref[0]
    flow = lax.dot_general(
        wave_ref[...], inj_ref[...], (((1,), (1,)), ((), ())), preferred_element_type=jnp.float32
    )
    current[...] = jnp.where(live, flow, 0.0)

    def prepare(x, _):
        for d in range(3):
            level = grades_ref[d, x]
            keep[d, x] = grade_table(level, absorb_keep)
            take[d, x] = grade_table(level, absorb_take)
        factor[x] = courant / eps_ref[x]
        return 0

    lax.fori_loop(0, depth_x, prepare, 0)
    for copy in loads:
        copy.wait()

    def pack_first(x):
        send_e[0, pl.ds(x, 1), :] = ef[0, x, 0:1, :]
        send_e[1, pl.ds(x, 1), :] = ef[2, x, 0:1, :]

    for x in range(depth_x):
        pack_first(x)
    peers = sum(present.astype(jnp.int32) for present in (has_left, has_right, has_down, has_up))
    pl.semaphore_wait(barrier, peers)

    def copies(kind):
        if kind == 0:
            return (
                (has_left, has_right, pltpu.make_async_remote_copy(
                    src_ref=ef.at[pl.ds(1, 2), 0], dst_ref=ef.at[pl.ds(1, 2), depth_x],
                    send_sem=send_sem.at[0], recv_sem=recv_sem.at[0],
                    device_id=(ix - 1, iy), device_id_type=MESH)),
                (has_down, has_up, pltpu.make_async_remote_copy(
                    src_ref=send_e, dst_ref=recv_e,
                    send_sem=send_sem.at[1], recv_sem=recv_sem.at[1],
                    device_id=(ix, iy - 1), device_id_type=MESH)),
            )
        return (
            (has_right, has_left, pltpu.make_async_remote_copy(
                src_ref=hf.at[pl.ds(1, 2), depth_x], dst_ref=hf.at[pl.ds(1, 2), 0],
                send_sem=send_sem.at[2], recv_sem=recv_sem.at[2],
                device_id=(ix + 1, iy), device_id_type=MESH)),
            (has_up, has_down, pltpu.make_async_remote_copy(
                src_ref=send_h, dst_ref=recv_h,
                send_sem=send_sem.at[3], recv_sem=recv_sem.at[3],
                device_id=(ix, iy + 1), device_id_type=MESH)),
        )

    def start(kind):
        for sends, _, copy in copies(kind):
            pl.when(sends)(copy.start)

    def finish(kind):
        for sends, receives, copy in copies(kind):
            pl.when(sends)(copy.wait_send)
            pl.when(receives)(copy.wait_recv)

    rows = lax.broadcasted_iota(jnp.int32, (depth_y, depth_z), 0)
    lanes = lax.broadcasted_iota(jnp.int32, (depth_y, depth_z), 1)

    def curl(x, here, beside, halo, memory, forward):
        turn_y = depth_y - 1 if forward else 1
        turn_z = depth_z - 1 if forward else 1
        edge_y = rows == (depth_y - 1 if forward else 0)
        edge_z = lanes == (depth_z - 1 if forward else 0)
        terms = []
        for number, (component, axis) in enumerate(derivative_pairs):
            value = here[component]
            if axis == 0:
                other = beside[component]
            elif axis == 1:
                line = halo[component // 2, pl.ds(x, 1), :]
                other = jnp.where(edge_y, line, pltpu.roll(value, turn_y, 0))
            else:
                other = jnp.where(edge_z, 0.0, pltpu.roll(value, turn_z, 1))
            slope = other - value if forward else value - other
            carried = keep[axis, x] * memory[number, x] + take[axis, x] * slope
            memory[number, x] = carried
            terms.append(slope + carried)
        return (terms[0] - terms[1], terms[2] - terms[3], terms[4] - terms[5])

    def update_h(block, _):
        for inner in range(UNROLL):
            x = block * UNROLL + inner
            here = [ef[c, x] for c in range(3)]
            beside = [None, ef[1, x + 1], ef[2, x + 1]]
            rotation = curl(x, here, beside, recv_e, me, True)
            fresh = [hf[c, x + 1] - courant * rotation[c] for c in range(3)]
            for c in range(3):
                hf[c, x + 1] = fresh[c]
            send_h[0, pl.ds(x, 1), :] = fresh[0][depth_y - 1:depth_y, :]
            send_h[1, pl.ds(x, 1), :] = fresh[2][depth_y - 1:depth_y, :]
        return 0

    def update_e(block, _):
        for inner in range(UNROLL):
            x = block * UNROLL + inner
            here = [hf[c, x + 1] for c in range(3)]
            beside = [None, hf[1, x], hf[2, x]]
            rotation = curl(x, here, beside, recv_h, mh, False)
            ratio = factor[x]
            fresh = [ef[c, x] + ratio * rotation[c] for c in range(3)]
            fresh[2] = fresh[2] - courant * source[x]
            for c in range(3):
                ef[c, x] = fresh[c]
            send_e[0, pl.ds(x, 1), :] = fresh[0][0:1, :]
            send_e[1, pl.ds(x, 1), :] = fresh[2][0:1, :]
        return 0

    def inject(step):
        high, low = split_two(current[pl.ds(step, 1), :])
        total = None
        for part in (high, low):
            piece = jnp.dot(
                cell_t[...] * part, depth[...], preferred_element_type=jnp.float32
            )
            total = piece if total is None else total + piece
        source[...] = total.reshape(source.shape)

    def read_out(step):
        values = ef[2, pl.ds(0, depth_x)].reshape(depth_x * depth_y, depth_z)
        high, low = split_two(values)
        picked = jnp.dot(high, depth_t[...], preferred_element_type=jnp.float32)
        picked = picked + jnp.dot(low, depth_t[...], preferred_element_type=jnp.float32)
        chosen = jnp.sum(picked * cell_f[...], axis=0, keepdims=True)
        record[pl.ds(step, 1), :] = chosen * current[pl.ds(step, 1), :]

    def turn(step, _):
        start(0)
        inject(step)
        finish(0)
        lax.fori_loop(0, depth_x // UNROLL, update_h, 0)
        start(1)
        read_out((step + steps - 1) % steps)
        finish(1)
        lax.fori_loop(0, depth_x // UNROLL, update_e, 0)
        return 0

    lax.fori_loop(0, steps, turn, 0)
    stores = [
        pltpu.make_async_copy(ef.at[:, pl.ds(0, depth_x)], e_out, store_sem.at[0]),
        pltpu.make_async_copy(hf.at[:, pl.ds(1, depth_x)], h_out, store_sem.at[1]),
    ]
    for copy in stores:
        copy.start()
    read_out(steps - 1)
    member = lax.broadcasted_iota(jnp.int32, (ports, slots), 0) == port_ref[...]
    member = jnp.where(member, 1.0, 0.0).astype(jnp.bfloat16)
    total = None
    for part in split_two(record[...]):
        piece = lax.dot_general(
            part, member, (((1,), (1,)), ((), ())), preferred_element_type=jnp.float32
        )
        total = piece if total is None else total + piece
    power_ref[...] = total
    for copy in stores:
        copy.wait()


def local(
    electric, magnetic, aux_electric, aux_magnetic, grades, permittivity,
    dipole_cell, dipole_port, live_count, injection, waveform,
):
    depth_x, depth_y, depth_z = permittivity.shape
    slots = dipole_cell.shape[1]
    ports, steps = waveform.shape
    block = (depth_x, depth_y, depth_z)
    cells = depth_x * depth_y
    f32 = jnp.float32
    vmem = pl.BlockSpec(memory_space=pltpu.VMEM)
    anywhere = pl.BlockSpec(memory_space=pl.ANY)
    electric, magnetic, power = pl.pallas_call(
        kernel,
        out_shape=(
            jax.ShapeDtypeStruct(electric.shape, f32),
            jax.ShapeDtypeStruct(magnetic.shape, f32),
            jax.ShapeDtypeStruct((steps, ports), f32),
        ),
        in_specs=[anywhere] * 4 + [vmem] * 4
        + [pl.BlockSpec(memory_space=pltpu.SMEM)] + [vmem] * 2,
        out_specs=(anywhere, anywhere, vmem),
        scratch_shapes=[
            pltpu.VMEM((3, depth_x + 1, depth_y, depth_z), f32),
            pltpu.VMEM((3, depth_x + 1, depth_y, depth_z), f32),
            pltpu.VMEM((6,) + block, f32),
            pltpu.VMEM((6,) + block, f32),
            pltpu.VMEM((3,) + block, f32),
            pltpu.VMEM((3,) + block, f32),
            pltpu.VMEM(block, f32),
            pltpu.VMEM(block, f32),
            pltpu.VMEM((2, depth_x, depth_z), f32),
            pltpu.VMEM((2, depth_x, depth_z), f32),
            pltpu.VMEM((2, depth_x, depth_z), f32),
            pltpu.VMEM((2, depth_x, depth_z), f32),
            pltpu.VMEM((cells, slots), jnp.bfloat16),
            pltpu.VMEM((cells, slots), f32),
            pltpu.VMEM((depth_z, slots), jnp.bfloat16),
            pltpu.VMEM((slots, depth_z), jnp.bfloat16),
            pltpu.VMEM((steps, slots), f32),
            pltpu.VMEM((steps, slots), f32),
            pltpu.SemaphoreType.DMA((4,)),
            pltpu.SemaphoreType.DMA((2,)),
            pltpu.SemaphoreType.DMA((4,)),
            pltpu.SemaphoreType.DMA((4,)),
        ],
        compiler_params=pltpu.CompilerParams(
            collective_id=0, has_side_effects=True, vmem_limit_bytes=40 * 1024 * 1024
        ),
    )(
        electric, magnetic, aux_electric, aux_magnetic, grades, permittivity,
        dipole_cell, dipole_port.reshape(1, slots), live_count, injection, waveform.T,
    )
    return electric, magnetic, lax.psum(power, ("gx", "gy"))


def solution(mesh):
    in_specs = (
        P(None, "gx", "gy", None),
        P(None, "gx", "gy", None),
        P(None, "gx", "gy", None),
        P(None, "gx", "gy", None),
        P(None, "gx", "gy", None),
        P("gx", "gy", None),
        P(None, ("gx", "gy")),
        P(("gx", "gy")),
        P(("gx", "gy")),
        P(("gx", "gy"), None),
        P(),
    )
    out_specs = (P(None, "gx", "gy", None), P(None, "gx", "gy", None), P())
    return jax.shard_map(local, mesh=mesh, in_specs=in_specs, out_specs=out_specs, check_vma=False)
```

```python
import functools

import jax
import jax.numpy as jnp
from jax import lax
from jax.experimental import pallas as pl
from jax.experimental.pallas import tpu as pltpu
from jax.sharding import PartitionSpec as P

MESH = pl.DeviceIdType.MESH
courant = 0.55
absorb_keep = (0.0, 0.92, 0.75, 0.45)
absorb_take = (0.0, -0.06, -0.18, -0.35)
derivative_pairs = ((2, 1), (1, 2), (0, 2), (2, 0), (1, 0), (0, 1))
UNROLL = 4


def grade_table(grades, table):
    result = jnp.where(grades == 1, table[1], 0.0)
    result = jnp.where(grades == 2, table[2], result)
    return jnp.where(grades == 3, table[3], result)


def split_two(values):
    high = values.astype(jnp.bfloat16)
    low = (values - high.astype(jnp.float32)).astype(jnp.bfloat16)
    return high, low


def kernel(
    e_in, h_in, me_in, mh_in, grades_ref, eps_ref, cell_ref, port_ref, live_ref, inj_ref, wave_ref,
    e_out, h_out, power_ref,
    ef, hf, me, mh, keep, take, factor, source,
    send_e, recv_e, send_h, recv_h, cell_t, cell_f, depth_t, depth, current, record,
    share, from_y, from_x, result,
    load_sem, store_sem, send_sem, recv_sem, send_sum, recv_sum,
):
    depth_x, depth_y, depth_z = eps_ref.shape
    ports, slots = inj_ref.shape[1], inj_ref.shape[0]
    steps = wave_ref.shape[0]
    ix, iy = lax.axis_index("gx"), lax.axis_index("gy")
    count_x, count_y = lax.axis_size("gx"), lax.axis_size("gy")
    has_left, has_right = ix > 0, ix < count_x - 1
    has_down, has_up = iy > 0, iy < count_y - 1

    loads = [
        pltpu.make_async_copy(e_in, ef.at[:, pl.ds(0, depth_x)], load_sem.at[0]),
        pltpu.make_async_copy(h_in, hf.at[:, pl.ds(1, depth_x)], load_sem.at[1]),
        pltpu.make_async_copy(me_in, me, load_sem.at[2]),
        pltpu.make_async_copy(mh_in, mh, load_sem.at[3]),
    ]
    for copy in loads:
        copy.start()

    plane = jnp.zeros((depth_y, depth_z), jnp.float32)
    for component in (1, 2):
        ef[component, depth_x] = plane
        hf[component, 0] = plane
    recv_e[...] = jnp.zeros(recv_e.shape, jnp.float32)
    recv_h[...] = jnp.zeros(recv_h.shape, jnp.float32)

    barrier = pltpu.get_barrier_semaphore()
    line_x = [(lax.rem(ix + offset, count_x), iy) for offset in range(1, count_x)]
    line_y = [(ix, lax.rem(iy + offset, count_y)) for offset in range(1, count_y)]
    for peer in line_x + line_y:
        pl.semaphore_signal(barrier, inc=1, device_id=peer, device_id_type=MESH)

    cells = (cell_ref[0:1, :] - ix * depth_x) * depth_y + (cell_ref[1:2, :] - iy * depth_y)
    hit = lax.broadcasted_iota(jnp.int32, cell_f.shape, 0) == cells
    cell_f[...] = jnp.where(hit, 1.0, 0.0)
    cell_t[...] = jnp.where(hit, 1.0, 0.0).astype(jnp.bfloat16)
    hit = lax.broadcasted_iota(jnp.int32, depth_t.shape, 0) == cell_ref[2:3, :]
    table = jnp.where(hit, 1.0, 0.0)
    depth_t[...] = table.astype(jnp.bfloat16)
    depth[...] = table.T.astype(jnp.bfloat16)
    live = lax.broadcasted_iota(jnp.int32, (1, slots), 1) < live_ref[0]
    flow = lax.dot_general(
        wave_ref[...], inj_ref[...], (((1,), (1,)), ((), ())), preferred_element_type=jnp.float32
    )
    current[...] = jnp.where(live, flow, 0.0)

    def prepare(x, _):
        for d in range(3):
            level = grades_ref[d, x]
            keep[d, x] = grade_table(level, absorb_keep)
            take[d, x] = grade_table(level, absorb_take)
        factor[x] = courant / eps_ref[x]
        return 0

    lax.fori_loop(0, depth_x, prepare, 0)
    for copy in loads:
        copy.wait()

    def pack_first(x):
        send_e[0, pl.ds(x, 1), :] = ef[0, x, 0:1, :]
        send_e[1, pl.ds(x, 1), :] = ef[2, x, 0:1, :]

    for x in range(depth_x):
        pack_first(x)
    pl.semaphore_wait(barrier, len(line_x) + len(line_y))

    def copies(kind):
        if kind == 0:
            return (
                (has_left, has_right, pltpu.make_async_remote_copy(
                    src_ref=ef.at[pl.ds(1, 2), 0], dst_ref=ef.at[pl.ds(1, 2), depth_x],
                    send_sem=send_sem.at[0], recv_sem=recv_sem.at[0],
                    device_id=(ix - 1, iy), device_id_type=MESH)),
                (has_down, has_up, pltpu.make_async_remote_copy(
                    src_ref=send_e, dst_ref=recv_e,
                    send_sem=send_sem.at[1], recv_sem=recv_sem.at[1],
                    device_id=(ix, iy - 1), device_id_type=MESH)),
            )
        return (
            (has_right, has_left, pltpu.make_async_remote_copy(
                src_ref=hf.at[pl.ds(1, 2), depth_x], dst_ref=hf.at[pl.ds(1, 2), 0],
                send_sem=send_sem.at[2], recv_sem=recv_sem.at[2],
                device_id=(ix + 1, iy), device_id_type=MESH)),
            (has_up, has_down, pltpu.make_async_remote_copy(
                src_ref=send_h, dst_ref=recv_h,
                send_sem=send_sem.at[3], recv_sem=recv_sem.at[3],
                device_id=(ix, iy + 1), device_id_type=MESH)),
        )

    def start(kind):
        for sends, _, copy in copies(kind):
            pl.when(sends)(copy.start)

    def finish(kind):
        for sends, receives, copy in copies(kind):
            pl.when(sends)(copy.wait_send)
            pl.when(receives)(copy.wait_recv)

    rows = lax.broadcasted_iota(jnp.int32, (depth_y, depth_z), 0)
    lanes = lax.broadcasted_iota(jnp.int32, (depth_y, depth_z), 1)

    def curl(x, here, beside, halo, memory, forward):
        turn_y = depth_y - 1 if forward else 1
        turn_z = depth_z - 1 if forward else 1
        edge_y = rows == (depth_y - 1 if forward else 0)
        edge_z = lanes == (depth_z - 1 if forward else 0)
        terms = []
        for number, (component, axis) in enumerate(derivative_pairs):
            value = here[component]
            if axis == 0:
                other = beside[component]
            elif axis == 1:
                line = halo[component // 2, pl.ds(x, 1), :]
                other = jnp.where(edge_y, line, pltpu.roll(value, turn_y, 0))
            else:
                other = jnp.where(edge_z, 0.0, pltpu.roll(value, turn_z, 1))
            slope = other - value if forward else value - other
            carried = keep[axis, x] * memory[number, x] + take[axis, x] * slope
            memory[number, x] = carried
            terms.append(slope + carried)
        return (terms[0] - terms[1], terms[2] - terms[3], terms[4] - terms[5])

    def update_h(block, _):
        for inner in range(UNROLL):
            x = block * UNROLL + inner
            here = [ef[c, x] for c in range(3)]
            beside = [None, ef[1, x + 1], ef[2, x + 1]]
            rotation = curl(x, here, beside, recv_e, me, True)
            fresh = [hf[c, x + 1] - courant * rotation[c] for c in range(3)]
            for c in range(3):
                hf[c, x + 1] = fresh[c]
            send_h[0, pl.ds(x, 1), :] = fresh[0][depth_y - 1:depth_y, :]
            send_h[1, pl.ds(x, 1), :] = fresh[2][depth_y - 1:depth_y, :]
        return 0

    def update_e(block, _):
        for inner in range(UNROLL):
            x = block * UNROLL + inner
            here = [hf[c, x + 1] for c in range(3)]
            beside = [None, hf[1, x], hf[2, x]]
            rotation = curl(x, here, beside, recv_h, mh, False)
            ratio = factor[x]
            fresh = [ef[c, x] + ratio * rotation[c] for c in range(3)]
            fresh[2] = fresh[2] - courant * source[x]
            for c in range(3):
                ef[c, x] = fresh[c]
            send_e[0, pl.ds(x, 1), :] = fresh[0][0:1, :]
            send_e[1, pl.ds(x, 1), :] = fresh[2][0:1, :]
        return 0

    def inject(step):
        high, low = split_two(current[pl.ds(step, 1), :])
        total = None
        for part in (high, low):
            piece = jnp.dot(
                cell_t[...] * part, depth[...], preferred_element_type=jnp.float32
            )
            total = piece if total is None else total + piece
        source[...] = total.reshape(source.shape)

    def read_out(step):
        values = ef[2, pl.ds(0, depth_x)].reshape(depth_x * depth_y, depth_z)
        high, low = split_two(values)
        picked = jnp.dot(high, depth_t[...], preferred_element_type=jnp.float32)
        picked = picked + jnp.dot(low, depth_t[...], preferred_element_type=jnp.float32)
        chosen = jnp.sum(picked * cell_f[...], axis=0, keepdims=True)
        record[pl.ds(step, 1), :] = chosen * current[pl.ds(step, 1), :]

    def turn(step, _):
        start(0)
        inject(step)
        finish(0)
        lax.fori_loop(0, depth_x // UNROLL, update_h, 0)
        start(1)
        read_out((step + steps - 1) % steps)
        finish(1)
        lax.fori_loop(0, depth_x // UNROLL, update_e, 0)
        return 0

    lax.fori_loop(0, steps, turn, 0)
    stores = [
        pltpu.make_async_copy(ef.at[:, pl.ds(0, depth_x)], e_out, store_sem.at[0]),
        pltpu.make_async_copy(hf.at[:, pl.ds(1, depth_x)], h_out, store_sem.at[1]),
    ]
    for copy in stores:
        copy.start()
    read_out(steps - 1)
    member = lax.broadcasted_iota(jnp.int32, (ports, slots), 0) == port_ref[...]
    member = jnp.where(member, 1.0, 0.0).astype(jnp.bfloat16)
    total = None
    for part in split_two(record[...]):
        piece = lax.dot_general(
            part, member, (((1,), (1,)), ((), ())), preferred_element_type=jnp.float32
        )
        total = piece if total is None else total + piece
    for row in range(steps):
        share[row] = total[row:row + 1, :]
    chunk = steps // count_y

    def spread(first, peers, source_of, target):
        moves = []
        for number, peer in enumerate(peers):
            moves.append(pltpu.make_async_remote_copy(
                src_ref=source_of(peer), dst_ref=target,
                send_sem=send_sum.at[first + number], recv_sem=recv_sum.at[first + number],
                device_id=peer, device_id_type=MESH))
            moves[-1].start()
        return moves

    def settle(moves):
        for move in moves:
            move.wait()

    mine = pl.ds(iy * chunk, chunk)
    moves = spread(
        0, line_y, lambda peer: share.at[pl.ds(peer[1] * chunk, chunk)], from_y.at[iy]
    )
    from_y[iy] = share[mine]
    settle(moves)
    from_x[ix] = sum(from_y[j] for j in range(count_y))
    first = len(line_y)
    settle(spread(first, line_x, lambda peer: from_x.at[ix], from_x.at[ix]))
    result[mine] = sum(from_x[i] for i in range(count_x))
    first = first + len(line_x)
    settle(spread(first, line_y, lambda peer: result.at[mine], result.at[mine]))
    for row in range(steps):
        power_ref[row:row + 1, :] = result[row]
    for copy in stores:
        copy.wait()


def local(
    electric, magnetic, aux_electric, aux_magnetic, grades, permittivity,
    dipole_cell, dipole_port, live_count, injection, waveform,
):
    depth_x, depth_y, depth_z = permittivity.shape
    slots = dipole_cell.shape[1]
    ports, steps = waveform.shape
    block = (depth_x, depth_y, depth_z)
    cells = depth_x * depth_y
    f32 = jnp.float32
    count_x, count_y = lax.axis_size("gx"), lax.axis_size("gy")
    chunk = steps // count_y
    assert chunk * count_y == steps
    transfers = count_x + 2 * count_y
    vmem = pl.BlockSpec(memory_space=pltpu.VMEM)
    anywhere = pl.BlockSpec(memory_space=pltpu.HBM)
    electric, magnetic, power = pl.pallas_call(
        kernel,
        out_shape=(
            jax.ShapeDtypeStruct(electric.shape, f32),
            jax.ShapeDtypeStruct(magnetic.shape, f32),
            jax.ShapeDtypeStruct((steps, ports), f32),
        ),
        in_specs=[anywhere] * 4 + [vmem] * 4
        + [pl.BlockSpec(memory_space=pltpu.SMEM)] + [vmem] * 2,
        out_specs=(anywhere, anywhere, vmem),
        scratch_shapes=[
            pltpu.VMEM((3, depth_x + 1, depth_y, depth_z), f32),
            pltpu.VMEM((3, depth_x + 1, depth_y, depth_z), f32),
            pltpu.VMEM((6,) + block, f32),
            pltpu.VMEM((6,) + block, f32),
            pltpu.VMEM((3,) + block, f32),
            pltpu.VMEM((3,) + block, f32),
            pltpu.VMEM(block, f32),
            pltpu.VMEM(block, f32),
            pltpu.VMEM((2, depth_x, depth_z), f32),
            pltpu.VMEM((2, depth_x, depth_z), f32),
            pltpu.VMEM((2, depth_x, depth_z), f32),
            pltpu.VMEM((2, depth_x, depth_z), f32),
            pltpu.VMEM((cells, slots), jnp.bfloat16),
            pltpu.VMEM((cells, slots), f32),
            pltpu.VMEM((depth_z, slots), jnp.bfloat16),
            pltpu.VMEM((slots, depth_z), jnp.bfloat16),
            pltpu.VMEM((steps, slots), f32),
            pltpu.VMEM((steps, slots), f32),
            pltpu.VMEM((steps, 1, ports), f32),
            pltpu.VMEM((count_y, chunk, 1, ports), f32),
            pltpu.VMEM((count_x, chunk, 1, ports), f32),
            pltpu.VMEM((steps, 1, ports), f32),
            pltpu.SemaphoreType.DMA((4,)),
            pltpu.SemaphoreType.DMA((2,)),
            pltpu.SemaphoreType.DMA((4,)),
            pltpu.SemaphoreType.DMA((4,)),
            pltpu.SemaphoreType.DMA((transfers,)),
            pltpu.SemaphoreType.DMA((transfers,)),
        ],
        compiler_params=pltpu.CompilerParams(
            collective_id=0, has_side_effects=True, vmem_limit_bytes=60 * 1024 * 1024
        ),
    )(
        electric, magnetic, aux_electric, aux_magnetic, grades, permittivity,
        dipole_cell, dipole_port.reshape(1, slots), live_count, injection, waveform.T,
    )
    return electric, magnetic, power


def solution(mesh):
    in_specs = (
        P(None, "gx", "gy", None),
        P(None, "gx", "gy", None),
        P(None, "gx", "gy", None),
        P(None, "gx", "gy", None),
        P(None, "gx", "gy", None),
        P("gx", "gy", None),
        P(None, ("gx", "gy")),
        P(("gx", "gy")),
        P(("gx", "gy")),
        P(("gx", "gy"), None),
        P(),
    )
    out_specs = (P(None, "gx", "gy", None), P(None, "gx", "gy", None), P())
    return jax.shard_map(local, mesh=mesh, in_specs=in_specs, out_specs=out_specs, check_vma=False)
```

```python
import functools

import jax
import jax.numpy as jnp
from jax import lax
from jax.experimental import pallas as pl
from jax.experimental.pallas import tpu as pltpu
from jax.sharding import PartitionSpec as P

MESH = pl.DeviceIdType.MESH
courant = 0.55
absorb_keep = (0.0, 0.92, 0.75, 0.45)
absorb_take = (0.0, -0.06, -0.18, -0.35)
derivative_pairs = ((2, 1), (1, 2), (0, 2), (2, 0), (1, 0), (0, 1))
UNROLL = 4


def grade_table(grades, table):
    result = jnp.where(grades == 1, table[1], 0.0)
    result = jnp.where(grades == 2, table[2], result)
    return jnp.where(grades == 3, table[3], result)


def split_two(values):
    high = values.astype(jnp.bfloat16)
    low = (values - high.astype(jnp.float32)).astype(jnp.bfloat16)
    return high, low


def kernel(
    e_in, h_in, me_in, mh_in, grades_ref, eps_ref, cell_ref, port_ref, live_ref, inj_ref, wave_ref,
    e_out, h_out, power_ref,
    ef, hf, me, mh, keep, take, factor, source,
    send_e, recv_e, send_h, recv_h, cell_t, cell_f, depth_t, depth, current, record,
    share, from_y, from_x, result,
    load_sem, store_sem, send_sem, recv_sem, send_sum, recv_sum,
):
    depth_x, depth_y, depth_z = eps_ref.shape
    ports, slots = inj_ref.shape[1], inj_ref.shape[0]
    steps = wave_ref.shape[0]
    ix, iy = lax.axis_index("gx"), lax.axis_index("gy")
    count_x, count_y = lax.axis_size("gx"), lax.axis_size("gy")
    has_left, has_right = ix > 0, ix < count_x - 1
    has_down, has_up = iy > 0, iy < count_y - 1

    loads = [
        pltpu.make_async_copy(e_in, ef.at[:, pl.ds(0, depth_x)], load_sem.at[0]),
        pltpu.make_async_copy(h_in, hf.at[:, pl.ds(1, depth_x)], load_sem.at[1]),
        pltpu.make_async_copy(me_in, me, load_sem.at[2]),
        pltpu.make_async_copy(mh_in, mh, load_sem.at[3]),
    ]
    for copy in loads:
        copy.start()

    plane = jnp.zeros((depth_y, depth_z), jnp.float32)
    for component in (1, 2):
        ef[component, depth_x] = plane
        hf[component, 0] = plane
    recv_e[...] = jnp.zeros(recv_e.shape, jnp.float32)
    recv_h[...] = jnp.zeros(recv_h.shape, jnp.float32)

    barrier = pltpu.get_barrier_semaphore()
    line_x = [(lax.rem(ix + offset, count_x), iy) for offset in range(1, count_x)]
    line_y = [(ix, lax.rem(iy + offset, count_y)) for offset in range(1, count_y)]
    for peer in line_x + line_y:
        pl.semaphore_signal(barrier, inc=1, device_id=peer, device_id_type=MESH)

    cells = (cell_ref[0:1, :] - ix * depth_x) * depth_y + (cell_ref[1:2, :] - iy * depth_y)
    hit = lax.broadcasted_iota(jnp.int32, cell_f.shape, 0) == cells
    cell_f[...] = jnp.where(hit, 1.0, 0.0)
    cell_t[...] = jnp.where(hit, 1.0, 0.0).astype(jnp.bfloat16)
    hit = lax.broadcasted_iota(jnp.int32, depth_t.shape, 0) == cell_ref[2:3, :]
    table = jnp.where(hit, 1.0, 0.0)
    depth_t[...] = table.astype(jnp.bfloat16)
    depth[...] = table.T.astype(jnp.bfloat16)
    live = lax.broadcasted_iota(jnp.int32, (1, slots), 1) < live_ref[0]
    flow = lax.dot_general(
        wave_ref[...], inj_ref[...], (((1,), (1,)), ((), ())), preferred_element_type=jnp.float32
    )
    current[...] = jnp.where(live, flow, 0.0)

    def prepare(x, _):
        for d in range(3):
            level = grades_ref[d, x]
            keep[d, x] = grade_table(level, absorb_keep)
            take[d, x] = grade_table(level, absorb_take)
        factor[x] = courant / eps_ref[x]
        return 0

    lax.fori_loop(0, depth_x, prepare, 0)
    for copy in loads:
        copy.wait()

    def pack_first(x):
        send_e[0, pl.ds(x, 1), :] = ef[0, x, 0:1, :]
        send_e[1, pl.ds(x, 1), :] = ef[2, x, 0:1, :]

    for x in range(depth_x):
        pack_first(x)
    pl.semaphore_wait(barrier, len(line_x) + len(line_y))

    def copies(kind):
        if kind == 0:
            return (
                (has_left, has_right, pltpu.make_async_remote_copy(
                    src_ref=ef.at[pl.ds(1, 2), 0], dst_ref=ef.at[pl.ds(1, 2), depth_x],
                    send_sem=send_sem.at[0], recv_sem=recv_sem.at[0],
                    device_id=(ix - 1, iy), device_id_type=MESH)),
                (has_down, has_up, pltpu.make_async_remote_copy(
                    src_ref=send_e, dst_ref=recv_e,
                    send_sem=send_sem.at[1], recv_sem=recv_sem.at[1],
                    device_id=(ix, iy - 1), device_id_type=MESH)),
            )
        return (
            (has_right, has_left, pltpu.make_async_remote_copy(
                src_ref=hf.at[pl.ds(1, 2), depth_x], dst_ref=hf.at[pl.ds(1, 2), 0],
                send_sem=send_sem.at[2], recv_sem=recv_sem.at[2],
                device_id=(ix + 1, iy), device_id_type=MESH)),
            (has_up, has_down, pltpu.make_async_remote_copy(
                src_ref=send_h, dst_ref=recv_h,
                send_sem=send_sem.at[3], recv_sem=recv_sem.at[3],
                device_id=(ix, iy + 1), device_id_type=MESH)),
        )

    def start(kind, side, wanted=True):
        sends, _, copy = copies(kind)[side]
        pl.when(jnp.logical_and(sends, wanted))(copy.start)

    def finish(kind):
        for sends, receives, copy in copies(kind):
            pl.when(sends)(copy.wait_send)
            pl.when(receives)(copy.wait_recv)

    rows = lax.broadcasted_iota(jnp.int32, (depth_y, depth_z), 0)
    lanes = lax.broadcasted_iota(jnp.int32, (depth_y, depth_z), 1)

    def curl(x, here, beside, halo, memory, forward):
        turn_y = depth_y - 1 if forward else 1
        turn_z = depth_z - 1 if forward else 1
        edge_y = rows == (depth_y - 1 if forward else 0)
        edge_z = lanes == (depth_z - 1 if forward else 0)
        terms = []
        for number, (component, axis) in enumerate(derivative_pairs):
            value = here[component]
            if axis == 0:
                other = beside[component]
            elif axis == 1:
                line = halo[component // 2, pl.ds(x, 1), :]
                other = jnp.where(edge_y, line, pltpu.roll(value, turn_y, 0))
            else:
                other = jnp.where(edge_z, 0.0, pltpu.roll(value, turn_z, 1))
            slope = other - value if forward else value - other
            carried = keep[axis, x] * memory[number, x] + take[axis, x] * slope
            memory[number, x] = carried
            terms.append(slope + carried)
        return (terms[0] - terms[1], terms[2] - terms[3], terms[4] - terms[5])

    def update_h(block, _):
        for inner in range(UNROLL):
            x = block * UNROLL + inner
            here = [ef[c, x] for c in range(3)]
            beside = [None, ef[1, x + 1], ef[2, x + 1]]
            rotation = curl(x, here, beside, recv_e, me, True)
            fresh = [hf[c, x + 1] - courant * rotation[c] for c in range(3)]
            for c in range(3):
                hf[c, x + 1] = fresh[c]
            send_h[0, pl.ds(x, 1), :] = fresh[0][depth_y - 1:depth_y, :]
            send_h[1, pl.ds(x, 1), :] = fresh[2][depth_y - 1:depth_y, :]
        return 0

    def update_e(block, _):
        for inner in range(UNROLL):
            x = block * UNROLL + inner
            here = [hf[c, x + 1] for c in range(3)]
            beside = [None, hf[1, x], hf[2, x]]
            rotation = curl(x, here, beside, recv_h, mh, False)
            ratio = factor[x]
            fresh = [ef[c, x] + ratio * rotation[c] for c in range(3)]
            fresh[2] = fresh[2] - courant * source[x]
            for c in range(3):
                ef[c, x] = fresh[c]
            send_e[0, pl.ds(x, 1), :] = fresh[0][0:1, :]
            send_e[1, pl.ds(x, 1), :] = fresh[2][0:1, :]
        return 0

    def inject(step):
        high, low = split_two(current[pl.ds(step, 1), :])
        total = None
        for part in (high, low):
            piece = jnp.dot(
                cell_t[...] * part, depth[...], preferred_element_type=jnp.float32
            )
            total = piece if total is None else total + piece
        source[...] = total.reshape(source.shape)

    def read_out(step):
        values = ef[2, pl.ds(0, depth_x)].reshape(depth_x * depth_y, depth_z)
        high, low = split_two(values)
        picked = jnp.dot(high, depth_t[...], preferred_element_type=jnp.float32)
        picked = picked + jnp.dot(low, depth_t[...], preferred_element_type=jnp.float32)
        chosen = jnp.sum(picked * cell_f[...], axis=0, keepdims=True)
        record[pl.ds(step, 1), :] = chosen * current[pl.ds(step, 1), :]

    blocks = depth_x // UNROLL

    def turn(step, _):
        inject(step)
        finish(0)
        update_h(blocks - 1, 0)
        start(1, 0)
        lax.fori_loop(0, blocks - 1, update_h, 0)
        start(1, 1)
        read_out((step + steps - 1) % steps)
        finish(1)
        more = step < steps - 1
        update_e(0, 0)
        start(0, 0, more)
        lax.fori_loop(1, blocks, update_e, 0)
        start(0, 1, more)
        return 0

    start(0, 1)
    start(0, 0)
    lax.fori_loop(0, steps, turn, 0)
    stores = [
        pltpu.make_async_copy(ef.at[:, pl.ds(0, depth_x)], e_out, store_sem.at[0]),
        pltpu.make_async_copy(hf.at[:, pl.ds(1, depth_x)], h_out, store_sem.at[1]),
    ]
    for copy in stores:
        copy.start()
    read_out(steps - 1)
    member = lax.broadcasted_iota(jnp.int32, (ports, slots), 0) == port_ref[...]
    member = jnp.where(member, 1.0, 0.0).astype(jnp.bfloat16)
    total = None
    for part in split_two(record[...]):
        piece = lax.dot_general(
            part, member, (((1,), (1,)), ((), ())), preferred_element_type=jnp.float32
        )
        total = piece if total is None else total + piece
    for row in range(steps):
        share[row] = total[row:row + 1, :]
    chunk = steps // count_y

    def spread(first, peers, source_of, target):
        moves = []
        for number, peer in enumerate(peers):
            moves.append(pltpu.make_async_remote_copy(
                src_ref=source_of(peer), dst_ref=target,
                send_sem=send_sum.at[first + number], recv_sem=recv_sum.at[first + number],
                device_id=peer, device_id_type=MESH))
            moves[-1].start()
        return moves

    def settle(moves):
        for move in moves:
            move.wait()

    mine = pl.ds(iy * chunk, chunk)
    moves = spread(
        0, line_y, lambda peer: share.at[pl.ds(peer[1] * chunk, chunk)], from_y.at[iy]
    )
    from_y[iy] = share[mine]
    settle(moves)
    from_x[ix] = sum(from_y[j] for j in range(count_y))
    first = len(line_y)
    settle(spread(first, line_x, lambda peer: from_x.at[ix], from_x.at[ix]))
    result[mine] = sum(from_x[i] for i in range(count_x))
    first = first + len(line_x)
    settle(spread(first, line_y, lambda peer: result.at[mine], result.at[mine]))
    for row in range(steps):
        power_ref[row:row + 1, :] = result[row]
    for copy in stores:
        copy.wait()


def local(
    electric, magnetic, aux_electric, aux_magnetic, grades, permittivity,
    dipole_cell, dipole_port, live_count, injection, waveform,
):
    depth_x, depth_y, depth_z = permittivity.shape
    slots = dipole_cell.shape[1]
    ports, steps = waveform.shape
    block = (depth_x, depth_y, depth_z)
    cells = depth_x * depth_y
    f32 = jnp.float32
    count_x, count_y = lax.axis_size("gx"), lax.axis_size("gy")
    chunk = steps // count_y
    assert chunk * count_y == steps
    transfers = count_x + 2 * count_y
    vmem = pl.BlockSpec(memory_space=pltpu.VMEM)
    anywhere = pl.BlockSpec(memory_space=pltpu.HBM)
    electric, magnetic, power = pl.pallas_call(
        kernel,
        out_shape=(
            jax.ShapeDtypeStruct(electric.shape, f32),
            jax.ShapeDtypeStruct(magnetic.shape, f32),
            jax.ShapeDtypeStruct((steps, ports), f32),
        ),
        in_specs=[anywhere] * 4 + [vmem] * 4
        + [pl.BlockSpec(memory_space=pltpu.SMEM)] + [vmem] * 2,
        out_specs=(anywhere, anywhere, vmem),
        scratch_shapes=[
            pltpu.VMEM((3, depth_x + 1, depth_y, depth_z), f32),
            pltpu.VMEM((3, depth_x + 1, depth_y, depth_z), f32),
            pltpu.VMEM((6,) + block, f32),
            pltpu.VMEM((6,) + block, f32),
            pltpu.VMEM((3,) + block, f32),
            pltpu.VMEM((3,) + block, f32),
            pltpu.VMEM(block, f32),
            pltpu.VMEM(block, f32),
            pltpu.VMEM((2, depth_x, depth_z), f32),
            pltpu.VMEM((2, depth_x, depth_z), f32),
            pltpu.VMEM((2, depth_x, depth_z), f32),
            pltpu.VMEM((2, depth_x, depth_z), f32),
            pltpu.VMEM((cells, slots), jnp.bfloat16),
            pltpu.VMEM((cells, slots), f32),
            pltpu.VMEM((depth_z, slots), jnp.bfloat16),
            pltpu.VMEM((slots, depth_z), jnp.bfloat16),
            pltpu.VMEM((steps, slots), f32),
            pltpu.VMEM((steps, slots), f32),
            pltpu.VMEM((steps, 1, ports), f32),
            pltpu.VMEM((count_y, chunk, 1, ports), f32),
            pltpu.VMEM((count_x, chunk, 1, ports), f32),
            pltpu.VMEM((steps, 1, ports), f32),
            pltpu.SemaphoreType.DMA((4,)),
            pltpu.SemaphoreType.DMA((2,)),
            pltpu.SemaphoreType.DMA((4,)),
            pltpu.SemaphoreType.DMA((4,)),
            pltpu.SemaphoreType.DMA((transfers,)),
            pltpu.SemaphoreType.DMA((transfers,)),
        ],
        compiler_params=pltpu.CompilerParams(
            collective_id=0, has_side_effects=True, vmem_limit_bytes=60 * 1024 * 1024
        ),
    )(
        electric, magnetic, aux_electric, aux_magnetic, grades, permittivity,
        dipole_cell, dipole_port.reshape(1, slots), live_count, injection, waveform.T,
    )
    return electric, magnetic, power


def solution(mesh):
    in_specs = (
        P(None, "gx", "gy", None),
        P(None, "gx", "gy", None),
        P(None, "gx", "gy", None),
        P(None, "gx", "gy", None),
        P(None, "gx", "gy", None),
        P("gx", "gy", None),
        P(None, ("gx", "gy")),
        P(("gx", "gy")),
        P(("gx", "gy")),
        P(("gx", "gy"), None),
        P(),
    )
    out_specs = (P(None, "gx", "gy", None), P(None, "gx", "gy", None), P())
    return jax.shard_map(local, mesh=mesh, in_specs=in_specs, out_specs=out_specs, check_vma=False)
```
